256 devices in a mesh: row: 4 (over x), col: 8 (over y, z_lo), layer: 8 (over z_hi, core).
Axes of the slice: x: 4, y: 4, z: 8 (z_hi: 4, z_lo: 2; z = z_hi * 2 + z_lo), core: 2. Of those that a mesh axis runs over, the one named last changes fastest.
Arguments:
- x_step: bfloat16 [6144, 6144], P(('col', 'layer'), 'row'), may hold values from -2 to 2, as said below
- density: bfloat16 [6144, 6144], P(('col', 'layer'), 'row'), may hold values from -12 to 12, as said below
- mask_x: int32 [48, 48], replicated, may hold values from 0 to 1, as said below
- mask_p: int32 [48, 48], replicated, may hold values from 0 to 1, as said below
- mask_c: int32 [48, 48], replicated, may hold values from 0 to 1, as said below
Outputs:
- updated: bfloat16 [6144, 6144], P(('col', 'layer'), 'row')
The draws below stay inside these ranges and needn't reach their ends.
Inputs may be any that keep to these rules, and one draw needn't show every extreme that they name: `x_step`: exactly antisymmetric. `density`: exactly symmetric. `mask_x`: symmetric 0/1 block pattern with every diagonal block set. `mask_p`: symmetric 0/1 block pattern with every diagonal block set. `mask_c`: symmetric 0/1 block pattern with every diagonal block set.
All inputs are finite; a program needn't handle non-finite values.
Results may differ from the reference program's by a relative error of at most 0.008.
Values may be sent and summed in bfloat16 or wider, within the bound.
No kernel may reach another device: no remote copies, remote signals or barrier semaphores. Data moves between devices by JAX's collectives and lax.ppermute only.
A program may use at most 64 MiB of HBM per device.

```python
import math
import jax
import jax.numpy as jnp

N = 6144
BLOCK = 128


def draw_base(key):
    return jax.random.normal(key, (N, N), jnp.float32)


def draw_x_step(key, part):
    base = draw_base(jax.random.fold_in(key, 11))
    return ((base - base.T) * (1.5 / math.sqrt(2.0 * N))).astype(jnp.bfloat16)


def draw_density(key, part):
    base = draw_base(jax.random.fold_in(key, 13))
    return ((base + base.T) * (1.0 / math.sqrt(2.0))).astype(jnp.bfloat16)


def block_pattern(key, percent):
    blocks = N // BLOCK
    drawn = jax.random.randint(key, (blocks, blocks), 0, 100)
    mirror = jnp.triu(drawn) + jnp.triu(drawn, 1).T
    kept = (mirror < percent).astype(jnp.int32)
    return jnp.maximum(kept, jnp.eye(blocks, dtype=jnp.int32))


def draw_mask_x(key, part):
    return block_pattern(jax.random.fold_in(key, 21), 48)


def draw_mask_p(key, part):
    return block_pattern(jax.random.fold_in(key, 23), 48)


def draw_mask_c(key, part):
    return block_pattern(jax.random.fold_in(key, 25), 64)


def setup_inputs(seed: int = 0) -> dict:
    key_list = jax.random.split(jax.random.key(seed), 6)
    return {
        "x_step": draw_x_step(jax.random.fold_in(key_list[5], 71), 0),
        "density": draw_density(jax.random.fold_in(key_list[5], 71), 0),
        "mask_x": draw_mask_x(jax.random.fold_in(key_list[5], 71), 0),
        "mask_p": draw_mask_p(jax.random.fold_in(key_list[5], 71), 0),
        "mask_c": draw_mask_c(jax.random.fold_in(key_list[5], 71), 0),
    }


def spread(pattern):
    return jnp.repeat(jnp.repeat(pattern, BLOCK, axis=0), BLOCK, axis=1)


def commutator(left, right, keep):
    forward = jnp.dot(left, right, preferred_element_type=jnp.float32)
    backward = jnp.dot(right, left, preferred_element_type=jnp.float32)
    return ((forward - backward) * keep).astype(jnp.bfloat16)


def reference(x_step, density, mask_x, mask_p, mask_c):
    x_kept = x_step * spread(mask_x).astype(jnp.bfloat16)
    p_kept = density * spread(mask_p).astype(jnp.bfloat16)
    keep_c = spread(mask_c).astype(jnp.float32)
    first = commutator(x_kept, p_kept, keep_c)
    second = commutator(x_kept, first, keep_c)
    total = p_kept.astype(jnp.float32) + first.astype(jnp.float32) + 0.5 * second.astype(jnp.float32)
    return total.astype(jnp.bfloat16)
```

```python
import jax
import jax.numpy as jnp
from jax import lax
from jax.sharding import PartitionSpec as P

BLOCKS = 48
NX, NY, NZ, NC = 4, 4, 8, 2
AXES = ("row", "col", "layer")


def flat(x, y, z, c):
    return ((x % NX) * 8 + (y % NY) * 2 + z % 2) * 8 + (z % NZ) // 2 * 2 + c


def pairs(move):
    return [
        (flat(x, y, z, c), flat(*move(x, y, z, c)))
        for x in range(NX)
        for y in range(NY)
        for z in range(NZ)
        for c in range(NC)
    ]


def to_x(a, s):
    return lax.ppermute(a, AXES, pairs(lambda x, y, z, c: (x + s, y, z, c)))


def to_y(a, s):
    return lax.ppermute(a, AXES, pairs(lambda x, y, z, c: (x, y + s, z, c)))


def to_z(a, s):
    return lax.ppermute(a, AXES, pairs(lambda x, y, z, c: (x, y, z + s, c)))


def to_core(a):
    return lax.ppermute(a, AXES, pairs(lambda x, y, z, c: (x, y, z, 1 - c)))


def to_mirror(a):
    return lax.ppermute(a, AXES, pairs(lambda x, y, z, c: (y, x, z, c)))


def expand(pattern, row_start, rows, col_block, width):
    block = NX * width // BLOCKS
    wide = BLOCKS // NX
    first = row_start // block
    picked = lax.dynamic_slice(
        jnp.concatenate([pattern, pattern[-1:]], 0), (first, col_block * wide), (2, wide)
    )
    lines = jnp.broadcast_to(picked[:, :, None], (2, wide, block)).reshape(2, width)
    inside = row_start + lax.broadcasted_iota(jnp.int32, (rows, width), 0) < (first + 1) * block
    return jnp.where(inside, lines[0:1], lines[1:2]).astype(jnp.float32)


def ring(block):
    half = block.shape[0] // 2
    up, down = block, block
    found = {0: block}
    for step in (1, 2, 3):
        up, down = to_z(up, 1), to_z(down, -1)
        found[NZ - step], found[step] = up, down
    found[4] = jnp.concatenate([to_z(up[:half], 1), to_z(down[half:], -1)], 0)
    return found


def collect(block, z, core):
    rows = block.shape[0]
    found = ring(block)
    out = jnp.zeros((NZ * NC * rows, block.shape[1]), block.dtype)
    for d in (0, 1, 7, 2, 6, 3, 5, 4):
        other = (z + d) % NZ
        base = (other % 2) * 8 + (other // 2) * 2
        out = lax.dynamic_update_slice(out, found[d], ((base + core) * rows, 0))
        out = lax.dynamic_update_slice(out, to_core(found[d]), ((base + 1 - core) * rows, 0))
    return out


def gather(block, send):
    return [block, send(block, -1), send(block, -2), send(block, -3)]


def scatter_sum(partial, send, here, line):
    rows = partial.shape[0] // 4

    def piece(s):
        return lax.dynamic_slice_in_dim(partial, (here + s - line) % 4 * rows, rows, 0)

    total = piece(0)
    for s in (1, 3, 2):
        total = total + send(piece(s).astype(jnp.bfloat16), s).astype(jnp.float32)
    return total


def dot_t(a, b):
    return lax.dot_general(a, b, (((1,), (1,)), ((), ())), preferred_element_type=jnp.float32)


def shards(x_step, density, mask_x, mask_p, mask_c):
    rows, width = x_step.shape
    x, col, layer = (lax.axis_index(a) for a in AXES)
    y, core = col // 2, layer % 2
    z = layer // 2 * 2 + col % 2
    start = (col * 8 + layer) * rows
    mirror_start = ((x * 2 + col % 2) * 8 + layer) * rows
    x_kept = x_step * expand(mask_x, start, rows, x, width).astype(jnp.bfloat16)
    p_kept = density * expand(mask_p, start, rows, x, width).astype(jnp.bfloat16)

    near = gather(jnp.concatenate([x_kept, p_kept], 0), to_y)
    near_x = jnp.concatenate([a[:rows] for a in near], 0)
    near_p = jnp.concatenate([a[rows:] for a in near], 0)
    tile_x = collect(x_kept, z, core)
    tile_p = collect(p_kept, z, core)
    partial = dot_t(near_p, tile_x) + dot_t(near_x, tile_p)
    total = scatter_sum(partial, to_x, x, y)
    first = (total * expand(mask_c, mirror_start, rows, y, width)).astype(jnp.bfloat16)

    mirror_x = jnp.concatenate(gather(to_mirror(x_kept), to_x), 0)
    near_first = jnp.concatenate(gather(first, to_x), 0)
    tile_first = collect(first, z, core)
    partial = dot_t(mirror_x, tile_first) - jnp.dot(
        near_first, tile_x, preferred_element_type=jnp.float32
    )
    total = scatter_sum(partial, to_y, y, x)
    second = (total * expand(mask_c, start, rows, x, width)).astype(jnp.bfloat16)
    result = (
        p_kept.astype(jnp.float32)
        + to_mirror(first).astype(jnp.float32)
        + 0.5 * second.astype(jnp.float32)
    )
    return result.astype(jnp.bfloat16)


def solution(mesh):
    in_specs = (P(("col", "layer"), "row"), P(("col", "layer"), "row"), P(), P(), P())
    out_specs = P(("col", "layer"), "row")
    return jax.shard_map(shards, mesh=mesh, in_specs=in_specs, out_specs=out_specs, check_vma=False)
```

```python
import functools

import jax
import jax.numpy as jnp
from jax import lax
from jax.experimental import pallas as pl
from jax.experimental.pallas import tpu as pltpu
from jax.sharding import PartitionSpec as P

BLOCKS = 48
NX, NY, NZ, NC = 4, 4, 8, 2
AXES = ("row", "col", "layer")


def flat(x, y, z, c):
    return ((x % NX) * 8 + (y % NY) * 2 + z % 2) * 8 + (z % NZ) // 2 * 2 + c


def pairs(move):
    return [
        (flat(x, y, z, c), flat(*move(x, y, z, c)))
        for x in range(NX)
        for y in range(NY)
        for z in range(NZ)
        for c in range(NC)
    ]


def to_x(a, s):
    return lax.ppermute(a, AXES, pairs(lambda x, y, z, c: (x + s, y, z, c)))


def to_y(a, s):
    return lax.ppermute(a, AXES, pairs(lambda x, y, z, c: (x, y + s, z, c)))


def to_z(a, s):
    return lax.ppermute(a, AXES, pairs(lambda x, y, z, c: (x, y, z + s, c)))


def to_core(a):
    return lax.ppermute(a, AXES, pairs(lambda x, y, z, c: (x, y, z, 1 - c)))


def to_mirror(a):
    return lax.ppermute(a, AXES, pairs(lambda x, y, z, c: (y, x, z, c)))


def lines_of(pattern, row_start, columns, block):
    padded = jnp.concatenate([pattern, pattern[-1:]], 0).astype(jnp.bfloat16)
    picked = lax.dynamic_slice(padded, (row_start // block, 0), (2, BLOCKS))
    chosen = columns[None, :] // block == lax.iota(jnp.int32, BLOCKS)[:, None]
    return jnp.dot(picked, chosen.astype(jnp.bfloat16), preferred_element_type=jnp.float32)


def expand(pattern, row_start, rows, columns, block):
    lines = lines_of(pattern, row_start, columns, block)
    place = row_start % block + lax.broadcasted_iota(jnp.int32, (rows, columns.shape[0]), 0)
    return jnp.where(place < block, lines[0:1], lines[1:2])


def ring(a, b):
    up = {"a": a, "b": b}
    down = dict(up)
    found = {"a": [a] + [None] * 7, "b": [b] + [None] * 7}
    for step in (1, 2, 3):
        for k in "ab":
            up[k], down[k] = to_z(up[k], 1), to_z(down[k], -1)
            found[k][NZ - step], found[k][step] = up[k], down[k]
    found["a"][4] = to_z(up["a"], 1)
    found["b"][4] = to_z(down["b"], -1)
    return found["a"], found["b"]


def after(value, *others):
    return lax.optimization_barrier((value, *others))[0]


def gather(block, send):
    return [block, send(block, -1), send(block, -2), send(block, -3)]


def dot_t(a, b):
    return lax.dot_general(a, b, (((1,), (1,)), ((), ())), preferred_element_type=jnp.float32)


def slot(z, d):
    there = lax.rem(z + d, NZ)
    return lax.rem(there, 2) * 4 + there // 2


def copy_all(copies, sems):
    started = [pltpu.make_async_copy(src, dst, sems.at[i]) for i, (src, dst) in enumerate(copies)]
    for c in started:
        c.start()
    for c in started:
        c.wait()


def first_kernel(rows, tile, info, near, near_other, *refs):
    xs, ps = refs[:NZ], refs[NZ : 2 * NZ]
    outs, tile_out = refs[2 * NZ : 2 * NZ + 4], refs[2 * NZ + 4]
    jx, jp, ix, ip, acc, sems, out_sem = refs[2 * NZ + 5 :]
    x, y, z, core = info[0], info[1], info[2], info[3]
    copies = []
    for r in range(4):
        for src, c in ((near, core), (near_other, 1 - core)):
            at = pl.ds(pl.multiple_of((2 * r + c) * rows, rows), rows)
            copies.append((src.at[pl.ds(2 * r * rows, rows)], jx.at[at]))
            copies.append((src.at[pl.ds((2 * r + 1) * rows, rows)], jp.at[at]))
    for d in range(NZ):
        at = pl.ds(pl.multiple_of(slot(z, d) * rows, rows), rows)
        copies.append((xs[d], ix.at[at]))
        copies.append((ps[d], ip.at[at]))
    copy_all(copies, sems)
    keep = pltpu.make_async_copy(ix, tile_out, out_sem)
    keep.start()

    @pl.loop(0, ix.shape[0] // tile)
    def _(n):
        at = pl.ds(pl.multiple_of(n * tile, tile), tile)
        acc[...] = dot_t(jp[...], ix[at]) + dot_t(jx[...], ip[at])
        for s in range(4):
            r = lax.rem(x + s - y + 4, 4)
            piece = acc[pl.ds(pl.multiple_of(r * 2 * rows, 2 * rows), 2 * rows)]
            outs[s][:, at] = piece.astype(outs[s].dtype)

    keep.wait()


def second_kernel(rows, tile, info, base, *refs):
    js, fa, fb = refs[:4], refs[4 : 4 + NZ], refs[4 + NZ : 4 + 2 * NZ]
    own_out, other_out = refs[4 + 2 * NZ : 6 + 2 * NZ]
    jx, fi, acc, sems = refs[6 + 2 * NZ :]
    z, core = info[2], info[3]
    copies = [(js[r], jx.at[pl.ds(2 * r * rows, 2 * rows)]) for r in range(4)]
    for d in range(NZ):
        for k, src in ((0, fa[d]), (1, fb[d])):
            at = pl.ds(pl.multiple_of((slot(z, d) * 2 + k) * rows, rows), rows)
            copies.append((src, fi.at[at]))
    copy_all(copies, sems)

    @pl.loop(0, fi.shape[0] // tile)
    def _(n):
        at = pl.ds(pl.multiple_of(n * tile, tile), tile)
        acc[...] = dot_t(jx[...], fi[at]) - base[:, at]
        for r in range(4):
            for out, c in ((own_out, core), (other_out, 1 - core)):
                piece = acc[pl.ds(pl.multiple_of((2 * r + c) * rows, rows), rows)]
                out[pl.ds(r * rows, rows), at] = piece.astype(out.dtype)


def first_product(info, near, near_other, xs, ps):
    rows, width = xs[0].shape
    half = width // 2
    tile = half // 3
    anywhere, vmem = pl.BlockSpec(memory_space=pl.ANY), pl.BlockSpec(memory_space=pltpu.VMEM)
    types = (jnp.float32, jnp.bfloat16, jnp.bfloat16, jnp.bfloat16)
    return pl.pallas_call(
        functools.partial(first_kernel, rows, tile),
        out_shape=[jax.ShapeDtypeStruct((2 * rows, half), t) for t in types]
        + [jax.ShapeDtypeStruct((half, width), jnp.bfloat16)],
        in_specs=[pl.BlockSpec(memory_space=pltpu.SMEM)] + [anywhere] * (2 + 2 * NZ),
        out_specs=[vmem] * 4 + [anywhere],
        scratch_shapes=[pltpu.VMEM((8 * rows, width), jnp.bfloat16) for _ in range(4)]
        + [
            pltpu.VMEM((8 * rows, tile), jnp.float32),
            pltpu.SemaphoreType.DMA((16 + 2 * NZ,)),
            pltpu.SemaphoreType.DMA,
        ],
        compiler_params=pltpu.CompilerParams(vmem_limit_bytes=40 * 2**20),
        cost_estimate=pl.CostEstimate(
            flops=4 * 8 * rows * half * width, bytes_accessed=12 * 2**20, transcendentals=0
        ),
        name="first_product",
    )(info, near, near_other, *xs, *ps)


def second_product(info, base, js, fa, fb):
    rows, half = fa[0].shape
    width = 2 * half
    tile = width // 6
    anywhere, vmem = pl.BlockSpec(memory_space=pl.ANY), pl.BlockSpec(memory_space=pltpu.VMEM)
    return pl.pallas_call(
        functools.partial(second_kernel, rows, tile),
        out_shape=[
            jax.ShapeDtypeStruct((4 * rows, width), t) for t in (jnp.float32, jnp.bfloat16)
        ],
        in_specs=[pl.BlockSpec(memory_space=pltpu.SMEM), vmem] + [anywhere] * (4 + 2 * NZ),
        out_specs=[vmem] * 2,
        scratch_shapes=[
            pltpu.VMEM((8 * rows, half), jnp.bfloat16),
            pltpu.VMEM((16 * rows, half), jnp.bfloat16),
            pltpu.VMEM((8 * rows, tile), jnp.float32),
            pltpu.SemaphoreType.DMA((4 + 2 * NZ,)),
        ],
        compiler_params=pltpu.CompilerParams(vmem_limit_bytes=40 * 2**20),
        cost_estimate=pl.CostEstimate(
            flops=2 * 8 * rows * half * width, bytes_accessed=12 * 2**20, transcendentals=0
        ),
        name="second_product",
    )(info, base, *js, *fa, *fb)


def shards(x_step, density, mask_x, mask_p, mask_c):
    rows, width = x_step.shape
    half = width // 2
    block = NX * width // BLOCKS
    x, col, layer = (lax.axis_index(a) for a in AXES)
    y, core = col // 2, layer % 2
    z = layer // 2 * 2 + col % 2
    info = jnp.stack([x, y, z, core]).astype(jnp.int32)
    start = (col * 8 + layer) * rows
    columns = x * width + lax.iota(jnp.int32, width)
    x_kept = x_step * expand(mask_x, start, rows, columns, block).astype(jnp.bfloat16)
    p_kept = density * expand(mask_p, start, rows, columns, block).astype(jnp.bfloat16)

    xs, ps = ring(x_kept, p_kept)
    both = after(jnp.concatenate([x_kept, p_kept], 0), ps[1], ps[7])
    near = jnp.concatenate(gather(both, to_y), 0)
    near_other = to_core(near)

    inner = lax.iota(jnp.int32, half)
    spread = (inner // rows * 2) * rows + inner % rows
    whole = lax.iota(jnp.int32, width)[None, :]
    mine = (whole == (spread + core * rows)[:, None]).astype(jnp.bfloat16)
    theirs = (whole == (spread + (1 - core) * rows)[:, None]).astype(jnp.bfloat16)

    mirror = to_mirror(after(x_kept, ps[2], ps[6]))
    mirror_mine = dot_t(mirror, mine).astype(jnp.bfloat16)
    mirror_got = to_core(dot_t(mirror, theirs).astype(jnp.bfloat16))
    stacked = jnp.where(
        core == 0,
        jnp.concatenate([mirror_mine, mirror_got], 0),
        jnp.concatenate([mirror_got, mirror_mine], 0),
    )
    mirrors = gather(stacked, to_x)

    own, *sent, tile_x = first_product(info, near, near_other, xs, ps)
    for s in (1, 3, 2):
        own = own + to_x(sent[s - 1], s).astype(jnp.float32)
    mirror_start = ((x * 2 + col % 2) * 8 + layer // 2 * 2) * rows
    mirror_columns = y * width + spread + core * rows
    keep = expand(mask_c, mirror_start, 2 * rows, mirror_columns, block)
    first = (own * keep).astype(jnp.bfloat16)

    fa, fb = ring(first[:rows], first[rows:])
    near_first = jnp.concatenate(gather(after(first, fb[1], fb[7]), to_x), 0)
    base = jnp.dot(near_first, tile_x, preferred_element_type=jnp.float32)

    turned = to_mirror(after(first, fb[2], fb[6]))
    turned_mine = lax.dynamic_slice_in_dim(turned, core * rows, rows, 0)
    turned_got = to_core(lax.dynamic_slice_in_dim(turned, (1 - core) * rows, rows, 0))
    first_here = jnp.dot(turned_mine, mine, preferred_element_type=jnp.float32) + jnp.dot(
        turned_got, theirs, preferred_element_type=jnp.float32
    )

    kept, other = second_product(info, base, mirrors, fa, fb)
    kept = kept + to_core(other).astype(jnp.float32)

    def piece(s):
        return lax.dynamic_slice_in_dim(kept, (y + s - x) % 4 * rows, rows, 0)

    total = piece(0)
    for s in (1, 3, 2):
        total = total + to_y(piece(s).astype(jnp.bfloat16), s).astype(jnp.float32)
    keep = expand(mask_c, start, rows, columns, block)
    second = (total * keep).astype(jnp.bfloat16)
    result = p_kept.astype(jnp.float32) + first_here + 0.5 * second.astype(jnp.float32)
    return result.astype(jnp.bfloat16)


def solution(mesh):
    in_specs = (P(("col", "layer"), "row"), P(("col", "layer"), "row"), P(), P(), P())
    out_specs = P(("col", "layer"), "row")
    return jax.shard_map(shards, mesh=mesh, in_specs=in_specs, out_specs=out_specs, check_vma=False)
```
